32 devices in a mesh: dp: 8 (over z, y), tensor: 4 (over x, core).
Axes of the slice: x: 2, y: 2, z: 4, core: 2. Of those that a mesh axis runs over, the one named last changes fastest.
Arguments:
- layer_input: float32 [6144, 2304], P(('dp', 'tensor')), may hold values from -6 to 6
- out_grad: float32 [6144, 2304], P(('dp', 'tensor')), may hold values from -6 to 6
- w_query: float32 [2304, 2048], P('dp', 'tensor'), may hold values from -0.5 to 0.5
- w_keyval: float32 [2304, 2, 1024], P('dp', None, 'tensor'), may hold values from -0.125 to 0.125
- w_output: float32 [2048, 2304], P('tensor', 'dp'), may hold values from -0.125 to 0.125
- w_gateup: float32 [2304, 2, 9216], P('dp', None, 'tensor'), may hold values from -0.125 to 0.125
- w_down: float32 [9216, 2304], P('tensor', 'dp'), may hold values from -0.0625 to 0.0625
- norm_scales: float32 [4, 2304], P(None, ('dp', 'tensor')), may hold values from -0.24 to 0.24
- momentum_query: float32 [2304, 2048], P('dp', 'tensor'), may hold values from -0.01171875 to 0.01171875
- momentum_keyval: float32 [2304, 2, 1024], P('dp', None, 'tensor'), may hold values from -0.01171875 to 0.01171875
- momentum_output: float32 [2048, 2304], P('tensor', 'dp'), may hold values from -0.01171875 to 0.01171875
- momentum_gateup: float32 [2304, 2, 9216], P('dp', None, 'tensor'), may hold values from -0.01171875 to 0.01171875
- momentum_down: float32 [9216, 2304], P('tensor', 'dp'), may hold values from -0.01171875 to 0.01171875
- momentum_scales: float32 [4, 2304], P(None, ('dp', 'tensor')), may hold values from -0.01171875 to 0.01171875
- variance_query: float32 [2304, 2048], P('dp', 'tensor'), may hold values from 2.6e-06 to 1.05e-05
- variance_keyval: float32 [2304, 2, 1024], P('dp', None, 'tensor'), may hold values from 2.6e-06 to 1.05e-05
- variance_output: float32 [2048, 2304], P('tensor', 'dp'), may hold values from 2.6e-06 to 1.05e-05
- variance_gateup: float32 [2304, 2, 9216], P('dp', None, 'tensor'), may hold values from 2.6e-06 to 1.05e-05
- variance_down: float32 [9216, 2304], P('tensor', 'dp'), may hold values from 2.6e-06 to 1.05e-05
- variance_scales: float32 [4, 2304], P(None, ('dp', 'tensor')), may hold values from 2.6e-06 to 1.05e-05
Outputs:
- layer_output: float32 [6144, 2304], P(('dp', 'tensor'))
- input_grad: float32 [6144, 2304], P(('dp', 'tensor'))
- grad_query: float32 [2304, 2048], P('dp', 'tensor')
- grad_keyval: float32 [2304, 2, 1024], P('dp', None, 'tensor')
- grad_output: float32 [2048, 2304], P('tensor', 'dp')
- grad_gateup: float32 [2304, 2, 9216], P('dp', None, 'tensor')
- grad_down: float32 [9216, 2304], P('tensor', 'dp')
- grad_scales: float32 [4, 2304], P(None, ('dp', 'tensor'))
- new_query: float32 [2304, 2048], P('dp', 'tensor')
- new_keyval: float32 [2304, 2, 1024], P('dp', None, 'tensor')
- new_output: float32 [2048, 2304], P('tensor', 'dp')
- new_gateup: float32 [2304, 2, 9216], P('dp', None, 'tensor')
- new_down: float32 [9216, 2304], P('tensor', 'dp')
- new_scales: float32 [4, 2304], P(None, ('dp', 'tensor'))
- new_momentum_query: float32 [2304, 2048], P('dp', 'tensor')
- new_momentum_keyval: float32 [2304, 2, 1024], P('dp', None, 'tensor')
- new_momentum_output: float32 [2048, 2304], P('tensor', 'dp')
- new_momentum_gateup: float32 [2304, 2, 9216], P('dp', None, 'tensor')
- new_momentum_down: float32 [9216, 2304], P('tensor', 'dp')
- new_momentum_scales: float32 [4, 2304], P(None, ('dp', 'tensor'))
- new_variance_query: float32 [2304, 2048], P('dp', 'tensor')
- new_variance_keyval: float32 [2304, 2, 1024], P('dp', None, 'tensor')
- new_variance_output: float32 [2048, 2304], P('tensor', 'dp')
- new_variance_gateup: float32 [2304, 2, 9216], P('dp', None, 'tensor')
- new_variance_down: float32 [9216, 2304], P('tensor', 'dp')
- new_variance_scales: float32 [4, 2304], P(None, ('dp', 'tensor'))
The draws below stay inside these ranges and needn't reach their ends.
All inputs are finite; a program needn't handle non-finite values.
Results may differ from the reference program's by a relative error of at most 0.02.
The reference program's roundings to bfloat16 on the way count: a program that leaves them out, or rounds other values in their place, can miss the bound.
Values may be sent and summed in bfloat16 or wider, within the bound.
No kernel may reach another device: no remote copies, remote signals or barrier semaphores. Data moves between devices by JAX's collectives and lax.ppermute only.
A program may use at most 320 MiB of HBM per device.

```python
import math
import jax
import jax.numpy as jnp
from jax import lax

D = 2304
FF = 9216
HQ = 8
HK = 4
HD = 256
SEQ = 768
TOKENS = 6144
N_DP = 8


def block_scale(stream_key, shape, shards, least, largest):
    gain = 1.0
    for position, shards_of in shards:
        steps = jax.random.uniform(jax.random.fold_in(jax.random.fold_in(stream_key, 6), position), (shards_of,), jnp.float32, least / len(shards), largest / len(shards))
        gain = gain * jnp.repeat(jnp.exp(steps), shape[position] // shards_of).reshape((-1,) + (1,) * (len(shape) - 1 - position))
    return gain


def centred(stream_key, dims, width, most, pieces=(), held_as=jnp.bfloat16):
    level = block_scale(stream_key, dims, pieces, -0.22, 0.18) if pieces else 1.0
    result = jax.random.normal(stream_key, dims, jnp.float32) * width * level
    return jnp.minimum(jnp.maximum(result, -most), most).astype(held_as)


def setup_inputs(seed: int = 0) -> dict:
    keys = jax.random.split(jax.random.key(seed), 21)
    layer_input = centred(keys[0], (TOKENS, D), 1.0, 6.0, ((0, 32),), jnp.float32)
    out_grad = centred(keys[1], (TOKENS, D), 1.0, 6.0, ((0, 32),), jnp.float32)
    w_query = centred(keys[2], (D, HQ * HD), 0.0833, 0.5, ((0, 8), (1, 4)), jnp.float32)
    w_keyval = centred(keys[3], (D, 2, HK * HD), D ** -0.5, 0.125, ((0, 8), (2, 4)), jnp.float32)
    w_output = centred(keys[4], (HQ * HD, D), (HQ * HD) ** -0.5, 0.125, ((0, 4), (1, 8)), jnp.float32)
    w_gateup = centred(keys[5], (D, 2, FF), D ** -0.5, 0.125, ((0, 8), (2, 4)), jnp.float32)
    w_down = centred(keys[6], (FF, D), FF ** -0.5, 0.0625, ((0, 4), (1, 8)), jnp.float32)
    norm_scales = centred(keys[7], (4, D), 0.04, 0.24, ((1, 32),), jnp.float32)
    momentum_query = centred(keys[8], (D, HQ * HD), 0.002, 0.01171875, ((0, 8), (1, 4)), jnp.float32)
    momentum_keyval = centred(keys[9], (D, 2, HK * HD), 0.002, 0.01171875, ((0, 8), (2, 4)), jnp.float32)
    momentum_output = centred(keys[10], (HQ * HD, D), 0.002, 0.01171875, ((0, 4), (1, 8)), jnp.float32)
    momentum_gateup = centred(keys[11], (D, 2, FF), 0.002, 0.01171875, ((0, 8), (2, 4)), jnp.float32)
    momentum_down = centred(keys[12], (FF, D), 0.002, 0.01171875, ((0, 4), (1, 8)), jnp.float32)
    momentum_scales = centred(keys[13], (4, D), 0.002, 0.01171875, ((1, 32),), jnp.float32)
    variance_query = jnp.clip(jnp.exp(math.log(1.049999991664663e-05) - 1.3958638 * jax.random.uniform(keys[14], (D, HQ * HD), jnp.float32) ** block_scale(keys[14], (D, HQ * HD), ((0, 8), (1, 4)), -0.2, 0.2)), 2.6000000161729986e-06, 1.049999991664663e-05)
    variance_keyval = jnp.clip(jnp.exp(math.log(1.049999991664663e-05) - 1.3958638 * jax.random.uniform(keys[15], (D, 2, HK * HD), jnp.float32) ** block_scale(keys[15], (D, 2, HK * HD), ((0, 8), (2, 4)), -0.2, 0.2)), 2.6000000161729986e-06, 1.049999991664663e-05)
    variance_output = jnp.clip(jnp.exp(math.log(1.049999991664663e-05) - 1.3958638 * jax.random.uniform(keys[16], (HQ * HD, D), jnp.float32) ** block_scale(keys[16], (HQ * HD, D), ((0, 4), (1, 8)), -0.2, 0.2)), 2.6000000161729986e-06, 1.049999991664663e-05)
    variance_gateup = jnp.clip(jnp.exp(math.log(1.049999991664663e-05) - 1.3958638 * jax.random.uniform(keys[17], (D, 2, FF), jnp.float32) ** block_scale(keys[17], (D, 2, FF), ((0, 8), (2, 4)), -0.2, 0.2)), 2.6000000161729986e-06, 1.049999991664663e-05)
    variance_down = jnp.clip(jnp.exp(math.log(1.049999991664663e-05) - 1.3958638 * jax.random.uniform(keys[18], (FF, D), jnp.float32) ** block_scale(keys[18], (FF, D), ((0, 4), (1, 8)), -0.2, 0.2)), 2.6000000161729986e-06, 1.049999991664663e-05)
    variance_scales = jnp.clip(jnp.exp(math.log(1.049999991664663e-05) - 1.3958638 * jax.random.uniform(keys[19], (4, D), jnp.float32) ** block_scale(keys[19], (4, D), ((1, 32),), -0.2, 0.2)), 2.6000000161729986e-06, 1.049999991664663e-05)
    return {"layer_input": layer_input, "out_grad": out_grad, "w_query": w_query, "w_keyval": w_keyval, "w_output": w_output, "w_gateup": w_gateup, "w_down": w_down, "norm_scales": norm_scales, "momentum_query": momentum_query, "momentum_keyval": momentum_keyval, "momentum_output": momentum_output, "momentum_gateup": momentum_gateup, "momentum_down": momentum_down, "momentum_scales": momentum_scales, "variance_query": variance_query, "variance_keyval": variance_keyval, "variance_output": variance_output, "variance_gateup": variance_gateup, "variance_down": variance_down, "variance_scales": variance_scales}


norm_eps = 1e-06
soft_cap = 50.0
gelu_coef = 0.7978845608028654
beta_one = 0.9
beta_two = 0.95
learn_rate = 0.01
decay_rate = 0.1
step_count = 3
adam_eps = 1e-08
clip_frac = 0.01

def product(form, left, right):
    return jnp.einsum(form, left.astype(jnp.float32), right.astype(jnp.float32), precision=lax.Precision.HIGHEST)

def rms_norm(values, gain_row):
    inverse = lax.rsqrt(lax.optimization_barrier(jnp.mean(values * values, axis=-1, keepdims=True)) + norm_eps)
    normed = values * inverse
    return (normed * (1.0 + gain_row), normed, inverse)

def norm_back(normed, inverse, gain_row, grad_out):
    grad_normed = grad_out * (1.0 + gain_row)
    grad_in = inverse * (grad_normed - normed * lax.optimization_barrier(jnp.mean(grad_normed * normed, axis=-1, keepdims=True)))
    return (grad_in, lax.optimization_barrier(jnp.sum(grad_out * normed, axis=0)))

def rotary_tables(length, head_dim):
    half_dim = head_dim // 2
    frequency = 10000.0 ** (-jnp.arange(half_dim, dtype=jnp.float32) / half_dim)
    angles = jnp.arange(length, dtype=jnp.float32)[:, None] * frequency[None, :]
    return (jnp.cos(angles)[:, None, :], jnp.sin(angles)[:, None, :])

def rotate(values, cosine, sine_table):
    half_dim = values.shape[-1] // 2
    first_half = values[..., :half_dim]
    second_half = values[..., half_dim:]
    return jnp.concatenate([first_half * cosine - second_half * sine_table, second_half * cosine + first_half * sine_table], axis=-1)

def rotate_back(values, cosine, sine_table):
    half_dim = values.shape[-1] // 2
    first_half = values[..., :half_dim]
    second_half = values[..., half_dim:]
    return jnp.concatenate([first_half * cosine + second_half * sine_table, second_half * cosine - first_half * sine_table], axis=-1)

def gelu_parts(gate_pre):
    inner_arg = gelu_coef * (gate_pre + 0.044715 * gate_pre * gate_pre * gate_pre)
    tanh_value = jnp.tanh(inner_arg)
    activated = 0.5 * gate_pre * (1.0 + tanh_value)
    gelu_slope = 0.5 * (1.0 + tanh_value) + 0.5 * gate_pre * (1.0 - tanh_value * tanh_value) * gelu_coef * (1.0 + 3.0 * 0.044715 * gate_pre * gate_pre)
    return (activated, gelu_slope)

def causal_scores(query_heads, key_rep):
    seq_len = query_heads.shape[0]
    raw_scores = product('qhd,khd->hqk', query_heads, key_rep)
    tanh_part = jnp.tanh(raw_scores / soft_cap)
    rows_idx = lax.broadcasted_iota(jnp.int32, (seq_len, seq_len), 0)
    cols_idx = lax.broadcasted_iota(jnp.int32, (seq_len, seq_len), 1)
    causal = (cols_idx <= rows_idx)[None]
    return (soft_cap * tanh_part, tanh_part, causal)

def attend(query_heads, key_heads, value_heads):
    group_size = query_heads.shape[1] // key_heads.shape[1]
    key_rep = jnp.repeat(key_heads, group_size, axis=1)
    value_rep = jnp.repeat(value_heads, group_size, axis=1)
    capped, tanh_part, causal = causal_scores(query_heads, key_rep)
    exp_total = lax.optimization_barrier(jnp.sum(jnp.where(causal, jnp.exp(capped), 0.0), axis=-1))
    log_total = jnp.log(exp_total)
    attn_probs = jnp.where(causal, jnp.exp(capped - log_total[..., None]), 0.0).astype(jnp.bfloat16)
    attn_out = product('hqk,khd->qhd', attn_probs, value_rep).astype(jnp.bfloat16)
    return (attn_out, log_total)

def attend_back(query_heads, key_heads, value_heads, attn_out, log_total, grad_attn):
    seq_len, heads_k, head_dim = key_heads.shape
    group_size = query_heads.shape[1] // heads_k
    key_rep = jnp.repeat(key_heads, group_size, axis=1)
    value_rep = jnp.repeat(value_heads, group_size, axis=1)
    capped, tanh_part, causal = causal_scores(query_heads, key_rep)
    attn_probs = jnp.where(causal, jnp.exp(capped - log_total[..., None]), 0.0)
    probs_low = attn_probs.astype(jnp.bfloat16)
    grad_probs = product('qhd,khd->hqk', grad_attn, value_rep)
    delta_rows = lax.optimization_barrier(jnp.sum(grad_attn.astype(jnp.float32) * attn_out.astype(jnp.float32), axis=-1))
    grad_raw = (attn_probs * (grad_probs - jnp.transpose(delta_rows)[:, :, None]) * (1.0 - tanh_part * tanh_part)).astype(jnp.bfloat16)
    grad_query = product('hqk,khd->qhd', grad_raw, key_rep)
    grad_key = product('hqk,qhd->khd', grad_raw, query_heads).reshape(seq_len, heads_k, group_size, head_dim).sum(axis=2)
    grad_value = product('hqk,qhd->khd', probs_low, grad_attn).reshape(seq_len, heads_k, group_size, head_dim).sum(axis=2)
    return (grad_query, grad_key, grad_value)

def adam_step(weight, moment, second, grad_now):
    moment_new = beta_one * moment + (1.0 - beta_one) * grad_now
    second_new = beta_two * second + (1.0 - beta_two) * grad_now * grad_now
    corrected = moment_new / (1.0 - beta_one ** step_count)
    divisor = jnp.sqrt(second_new / (1.0 - beta_two ** step_count)) + adam_eps
    weight_new = weight - learn_rate * (corrected / divisor + decay_rate * weight)
    return (weight_new, moment_new, second_new)

def clip_grad(grad_now, entries):
    limit = clip_frac * math.sqrt(entries)
    total = jnp.sqrt(jnp.sum(grad_now * grad_now))
    return grad_now * (limit / jnp.maximum(total, limit))

def reference(layer_input, out_grad, w_query, w_keyval, w_output, w_gateup, w_down, norm_scales, momentum_query, momentum_keyval, momentum_output, momentum_gateup, momentum_down, momentum_scales, variance_query, variance_keyval, variance_output, variance_gateup, variance_down, variance_scales):
    low_query = w_query.astype(jnp.bfloat16)
    low_keyval = w_keyval.reshape(D, 2 * HK * HD).astype(jnp.bfloat16)
    low_output = w_output.astype(jnp.bfloat16)
    low_gateup = w_gateup.reshape(D, 2 * FF).astype(jnp.bfloat16)
    low_down = w_down.astype(jnp.bfloat16)
    low_qkv = jnp.concatenate([low_query, low_keyval], axis=1)
    query_mult = 1.0 / math.sqrt(HD)
    cosine, sine_table = rotary_tables(SEQ, HD)
    kv_width = HK * HD

    def one_sequence(carry, pair):
        seq_in, seq_grad = pair
        normed_in, unit_in, inv_in = rms_norm(seq_in, norm_scales[0])
        attn_in = normed_in.astype(jnp.bfloat16)
        query_raw = jnp.dot(attn_in, low_query, preferred_element_type=jnp.float32)
        query_heads = (rotate(query_raw.reshape(SEQ, HQ, HD), cosine, sine_table) * query_mult).astype(jnp.bfloat16)
        keyval_raw = jnp.dot(attn_in, low_keyval, preferred_element_type=jnp.float32)
        key_heads = rotate(keyval_raw[:, :kv_width].reshape(SEQ, HK, HD), cosine, sine_table).astype(jnp.bfloat16)
        value_heads = keyval_raw[:, kv_width:].reshape(SEQ, HK, HD).astype(jnp.bfloat16)
        attn_out, log_total = attend(query_heads, key_heads, value_heads)
        attn_flat = attn_out.reshape(SEQ, HQ * HD)
        mixed = jnp.dot(attn_flat, low_output, preferred_element_type=jnp.float32)
        post_attn, unit_mix, inv_mix = rms_norm(mixed, norm_scales[1])
        residual = seq_in + post_attn
        normed_ff, unit_ff, inv_ff = rms_norm(residual, norm_scales[2])
        ffn_in = normed_ff.astype(jnp.bfloat16)
        gate_up = jnp.dot(ffn_in, low_gateup, preferred_element_type=jnp.float32)
        gate_pre = gate_up[:, :FF]
        up_pre = gate_up[:, FF:]
        activated, gelu_slope = gelu_parts(gate_pre)
        hidden = (activated * up_pre).astype(jnp.bfloat16)
        ffn_out = jnp.dot(hidden, low_down, preferred_element_type=jnp.float32)
        post_ffn, unit_ffn, inv_ffn = rms_norm(ffn_out, norm_scales[3])
        seq_out = residual + post_ffn
        grad_ffn, scale_three = norm_back(unit_ffn, inv_ffn, norm_scales[3], seq_grad)
        grad_ffn_low = grad_ffn.astype(jnp.bfloat16)
        down_part = jnp.dot(hidden.T, grad_ffn_low, preferred_element_type=jnp.float32)
        grad_hidden = jnp.dot(grad_ffn_low, low_down.T, preferred_element_type=jnp.float32)
        grad_gate = (grad_hidden * up_pre * gelu_slope).astype(jnp.bfloat16)
        grad_up = (grad_hidden * activated).astype(jnp.bfloat16)
        grad_gu = jnp.concatenate([grad_gate, grad_up], axis=1)
        gateup_part = jnp.dot(ffn_in.T, grad_gu, preferred_element_type=jnp.float32)
        grad_normed_ff = jnp.dot(grad_gu, low_gateup.T, preferred_element_type=jnp.float32)
        grad_res_ff, scale_two = norm_back(unit_ff, inv_ff, norm_scales[2], grad_normed_ff)
        grad_residual = seq_grad + grad_res_ff
        grad_mixed, scale_one = norm_back(unit_mix, inv_mix, norm_scales[1], grad_residual)
        grad_mixed_low = grad_mixed.astype(jnp.bfloat16)
        output_part = jnp.dot(attn_flat.T, grad_mixed_low, preferred_element_type=jnp.float32)
        grad_attn = jnp.dot(grad_mixed_low, low_output.T, preferred_element_type=jnp.float32).astype(jnp.bfloat16).reshape(SEQ, HQ, HD)
        grad_q, grad_k, grad_v = attend_back(query_heads, key_heads, value_heads, attn_out, log_total, grad_attn)
        grad_q_raw = rotate_back(grad_q * query_mult, cosine, sine_table).astype(jnp.bfloat16).reshape(SEQ, HQ * HD)
        grad_k_raw = rotate_back(grad_k, cosine, sine_table).astype(jnp.bfloat16).reshape(SEQ, kv_width)
        grad_v_raw = grad_v.astype(jnp.bfloat16).reshape(SEQ, kv_width)
        grad_kv = jnp.concatenate([grad_k_raw, grad_v_raw], axis=1)
        query_part = jnp.dot(attn_in.T, grad_q_raw, preferred_element_type=jnp.float32)
        keyval_part = jnp.dot(attn_in.T, grad_kv, preferred_element_type=jnp.float32)
        grad_qkv = jnp.concatenate([grad_q_raw, grad_kv], axis=1)
        grad_normed_in = jnp.dot(grad_qkv, low_qkv.T, preferred_element_type=jnp.float32)
        grad_in_norm, scale_zero = norm_back(unit_in, inv_in, norm_scales[0], grad_normed_in)
        seq_in_grad = grad_residual + grad_in_norm
        scale_part = jnp.stack([scale_zero, scale_one, scale_two, scale_three])
        sum_q, sum_kv, sum_o, sum_gu, sum_d, sum_s = carry
        new_carry = (sum_q + query_part, sum_kv + keyval_part, sum_o + output_part, sum_gu + gateup_part, sum_d + down_part, sum_s + scale_part)
        return (new_carry, (seq_out, seq_in_grad))
    init = (jnp.zeros((D, HQ * HD), jnp.float32), jnp.zeros((D, 2 * kv_width), jnp.float32), jnp.zeros((HQ * HD, D), jnp.float32), jnp.zeros((D, 2 * FF), jnp.float32), jnp.zeros((FF, D), jnp.float32), jnp.zeros((4, D), jnp.float32))
    sums, (outs_seq, grads_seq) = lax.scan(one_sequence, init, (layer_input.reshape(N_DP, SEQ, D), out_grad.reshape(N_DP, SEQ, D)))
    grad_query = sums[0]
    grad_keyval = sums[1].reshape(D, 2, kv_width)
    grad_output = sums[2]
    grad_gateup = sums[3].reshape(D, 2, FF)
    grad_down = sums[4]
    grad_scales = sums[5]
    new_q = adam_step(w_query, momentum_query, variance_query, clip_grad(grad_query, D * HQ * HD))
    new_kv = adam_step(w_keyval, momentum_keyval, variance_keyval, clip_grad(grad_keyval, D * 2 * HK * HD))
    new_o = adam_step(w_output, momentum_output, variance_output, clip_grad(grad_output, HQ * HD * D))
    new_gu = adam_step(w_gateup, momentum_gateup, variance_gateup, clip_grad(grad_gateup, D * 2 * FF))
    new_d = adam_step(w_down, momentum_down, variance_down, clip_grad(grad_down, FF * D))
    new_s = adam_step(norm_scales, momentum_scales, variance_scales, clip_grad(grad_scales, 4 * D))
    return (outs_seq.reshape(N_DP * SEQ, D), grads_seq.reshape(N_DP * SEQ, D), grad_query, grad_keyval, grad_output, grad_gateup, grad_down, grad_scales, new_q[0], new_kv[0], new_o[0], new_gu[0], new_d[0], new_s[0], new_q[1], new_kv[1], new_o[1], new_gu[1], new_d[1], new_s[1], new_q[2], new_kv[2], new_o[2], new_gu[2], new_d[2], new_s[2])
```

```python
import math

import jax
import jax.numpy as jnp
import numpy as np
from jax import lax
from jax.sharding import PartitionSpec as P

D = 2304
FF = 9216
HQ = 8
HK = 4
HD = 256


norm_eps = 1e-06
soft_cap = 50.0
gelu_coef = 0.7978845608028654
beta_one = 0.9
beta_two = 0.95
learn_rate = 0.01
decay_rate = 0.1
step_count = 3
adam_eps = 1e-08
clip_frac = 0.01


low = jnp.bfloat16
wide = jnp.float32


def rms_norm(values, gain_row):
    inverse = lax.rsqrt(jnp.mean(values * values, axis=-1, keepdims=True) + norm_eps)
    normed = values * inverse
    return (normed * (1.0 + gain_row), normed, inverse)


def norm_back(normed, inverse, gain_row, grad_out):
    grad_normed = grad_out * (1.0 + gain_row)
    grad_in = inverse * (
        grad_normed - normed * jnp.mean(grad_normed * normed, axis=-1, keepdims=True)
    )
    return (grad_in, jnp.sum(grad_out * normed, axis=0))


def rotate(values, cosine, sine_table):
    half_dim = values.shape[-1] // 2
    first_half = values[..., :half_dim]
    second_half = values[..., half_dim:]
    return jnp.concatenate(
        [
            first_half * cosine - second_half * sine_table,
            second_half * cosine + first_half * sine_table,
        ],
        axis=-1,
    )


def rotate_back(values, cosine, sine_table):
    return rotate(values, cosine, -sine_table)


def gelu_parts(gate_pre):
    inner_arg = gelu_coef * (gate_pre + 0.044715 * gate_pre * gate_pre * gate_pre)
    tanh_value = jnp.tanh(inner_arg)
    activated = 0.5 * gate_pre * (1.0 + tanh_value)
    gelu_slope = 0.5 * (1.0 + tanh_value) + 0.5 * gate_pre * (
        1.0 - tanh_value * tanh_value
    ) * gelu_coef * (1.0 + 3.0 * 0.044715 * gate_pre * gate_pre)
    return (activated, gelu_slope)


def causal_scores(query_heads, key_rep, causal):
    raw_scores = jnp.einsum(
        "qhd,khd->hqk", query_heads, key_rep, preferred_element_type=wide
    )
    tanh_part = jnp.tanh(raw_scores / soft_cap)
    return (soft_cap * tanh_part, tanh_part)


def attend(query_heads, key_heads, value_heads, causal):
    group_size = query_heads.shape[1] // key_heads.shape[1]
    key_rep = jnp.repeat(key_heads, group_size, axis=1)
    value_rep = jnp.repeat(value_heads, group_size, axis=1)
    capped, tanh_part = causal_scores(query_heads, key_rep, causal)
    exp_total = jnp.sum(jnp.where(causal, jnp.exp(capped), 0.0), axis=-1)
    log_total = jnp.log(exp_total)
    attn_probs = jnp.where(causal, jnp.exp(capped - log_total[..., None]), 0.0).astype(low)
    attn_out = jnp.einsum(
        "hqk,khd->qhd", attn_probs, value_rep, preferred_element_type=wide
    ).astype(low)
    return (attn_out, log_total)


def attend_back(query_heads, key_heads, value_heads, attn_out, log_total, grad_attn, causal):
    seq_len, heads_k, head_dim = key_heads.shape
    group_size = query_heads.shape[1] // heads_k
    key_rep = jnp.repeat(key_heads, group_size, axis=1)
    value_rep = jnp.repeat(value_heads, group_size, axis=1)
    capped, tanh_part = causal_scores(query_heads, key_rep, causal)
    attn_probs = jnp.where(causal, jnp.exp(capped - log_total[..., None]), 0.0)
    probs_low = attn_probs.astype(low)
    grad_probs = jnp.einsum("qhd,khd->hqk", grad_attn, value_rep, preferred_element_type=wide)
    delta_rows = jnp.sum(grad_attn.astype(wide) * attn_out.astype(wide), axis=-1)
    grad_raw = (
        attn_probs
        * (grad_probs - jnp.transpose(delta_rows)[:, :, None])
        * (1.0 - tanh_part * tanh_part)
    ).astype(low)
    grad_query = jnp.einsum("hqk,khd->qhd", grad_raw, key_rep, preferred_element_type=wide)
    grad_key = (
        jnp.einsum("hqk,qhd->khd", grad_raw, query_heads, preferred_element_type=wide)
        .reshape(seq_len, heads_k, group_size, head_dim)
        .sum(axis=2)
    )
    grad_value = (
        jnp.einsum("hqk,qhd->khd", probs_low, grad_attn, preferred_element_type=wide)
        .reshape(seq_len, heads_k, group_size, head_dim)
        .sum(axis=2)
    )
    return (grad_query, grad_key, grad_value)


def adam_step(weight, moment, second, grad_now):
    moment_new = beta_one * moment + (1.0 - beta_one) * grad_now
    second_new = beta_two * second + (1.0 - beta_two) * grad_now * grad_now
    corrected = moment_new / (1.0 - beta_one**step_count)
    divisor = jnp.sqrt(second_new / (1.0 - beta_two**step_count)) + adam_eps
    weight_new = weight - learn_rate * (corrected / divisor + decay_rate * weight)
    return (weight_new, moment_new, second_new)


def clip_with(grad_now, squared, entries):
    limit = clip_frac * math.sqrt(entries)
    total = jnp.sqrt(squared)
    return grad_now * (limit / jnp.maximum(total, limit))


def dot(left, right):
    return jnp.dot(left, right, preferred_element_type=wide)


def dot_bt(left, right):
    return lax.dot_general(left, right, (((1,), (1,)), ((), ())), preferred_element_type=wide)


def dot_at(left, right):
    return lax.dot_general(left, right, (((0,), (0,)), ((), ())), preferred_element_type=wide)


def square_sum(value):
    return jnp.sum(value * value)


class Wires:
    def __init__(self, mesh):
        self.n = mesh.shape["dp"]
        self.t = mesh.shape["tensor"]
        ring = list(range(0, self.n, 2)) + list(range(self.n - 1, 0, -2))
        place = [0] * self.n
        for spot, device in enumerate(ring):
            place[device] = spot
        self.ring = np.array(ring, np.int32)
        self.place = np.array(place, np.int32)
        self.up = [(ring[i], ring[(i + 1) % self.n]) for i in range(self.n)]
        self.down = [(b, a) for a, b in self.up]

    def pairs(self, way):
        return self.up if way > 0 else self.down

    def at(self, offset):
        spot = jnp.asarray(self.place)[lax.axis_index("dp")]
        return jnp.asarray(self.ring)[(spot + offset) % self.n]

    def hops(self, long_up):
        longer = self.n // 2
        shorter = self.n - 1 - longer
        return (longer, shorter) if long_up else (shorter, longer)

    def gather(self, shard, long_up):
        rows, columns = shard.shape
        full = jnp.zeros((self.n, rows, columns), shard.dtype)
        full = lax.dynamic_update_slice(full, shard[None], (lax.axis_index("dp"), 0, 0))
        ups, downs = self.hops(long_up)
        going = {1: shard, -1: shard}
        for step in range(1, max(ups, downs) + 1):
            for way, most in ((1, ups), (-1, downs)):
                if step <= most:
                    going[way] = lax.ppermute(going[way], "dp", self.pairs(way))
                    full = lax.dynamic_update_slice(
                        full, going[way][None], (self.at(-way * step), 0, 0)
                    )
        return full.reshape(self.n * rows, columns)

    def scatter(self, whole, long_up):
        parts = whole.reshape(self.n, whole.shape[0] // self.n, whole.shape[1])

        def block(index):
            return lax.dynamic_index_in_dim(parts, index, 0, keepdims=False)

        ups, downs = self.hops(long_up)
        total = block(lax.axis_index("dp")).astype(wide)
        for way, most in ((1, ups), (-1, downs)):
            sent = block(self.at(way * most))
            for left in range(most - 1, 0, -1):
                got = lax.ppermute(sent, "dp", self.pairs(way))
                sent = (got.astype(wide) + block(self.at(way * left)).astype(wide)).astype(low)
            total = total + lax.ppermute(sent, "dp", self.pairs(way)).astype(wide)
        return total

    def swap(self, value, bit):
        return lax.ppermute(value, "tensor", [(i, i ^ bit) for i in range(self.t)])

    def swap_dp(self, value, bit):
        return lax.ppermute(value, "dp", [(i, i ^ bit) for i in range(self.n)])

    def sum_all(self, value):
        bit = 1
        while bit < self.t:
            value = value + self.swap(value, bit)
            bit *= 2
        bit = 1
        while bit < self.n:
            value = value + self.swap_dp(value, bit)
            bit *= 2
        return value

    def rows_all(self, mine):
        across = self.swap(mine, 2)
        near = jnp.concatenate([mine, self.swap(mine, 1)], axis=0)
        far = jnp.concatenate([across, self.swap(across, 1)], axis=0)
        return near, far

    def rows_sum(self, near, far):
        half = near.shape[0] // 2
        for_across = far[:half] + self.swap(far[half:].astype(low), 1).astype(wide)
        across = self.swap(for_across.astype(low), 2).astype(wide)
        mine = near[:half] + self.swap(near[half:].astype(low), 1).astype(wide)
        return mine + across


def make_body(mesh):
    wires = Wires(mesh)

    def body(
        layer_input,
        out_grad,
        w_query,
        w_keyval,
        w_output,
        w_gateup,
        w_down,
        norm_scales,
        momentum_query,
        momentum_keyval,
        momentum_output,
        momentum_gateup,
        momentum_down,
        momentum_scales,
        variance_query,
        variance_keyval,
        variance_output,
        variance_gateup,
        variance_down,
        variance_scales,
    ):
        local_rows, model_dim = layer_input.shape
        depth = w_query.shape[0]
        q_width = w_query.shape[1]
        kv_width = w_keyval.shape[2]
        f_width = w_gateup.shape[2]
        qkv_shard = jnp.concatenate(
            [w_query, w_keyval.reshape(depth, 2 * kv_width)], axis=1
        ).astype(low)
        full_qkv = wires.gather(qkv_shard, True)
        full_out = wires.gather(jnp.transpose(w_output.astype(low)), False)
        full_gate = wires.gather(w_gateup[:, 0, :].astype(low), True)
        full_up = wires.gather(w_gateup[:, 1, :].astype(low), False)
        full_down = wires.gather(jnp.transpose(w_down.astype(low)), True)

        my_index = lax.axis_index("dp") * wires.t + lax.axis_index("tensor")
        scale_width = norm_scales.shape[1]
        scales = wires.sum_all(
            lax.dynamic_update_slice(
                jnp.zeros((norm_scales.shape[0], model_dim), wide),
                norm_scales,
                (0, my_index * scale_width),
            )
        )
        query_mult = 1.0 / math.sqrt(HD)

        my_tensor = lax.axis_index("tensor")
        seq_len = local_rows * wires.t
        within = jnp.arange(local_rows, dtype=jnp.int32)
        positions = jnp.concatenate(
            [(my_tensor ^ j) * local_rows + within for j in range(wires.t)]
        )
        half_dim = HD // 2
        frequency = 10000.0 ** (-jnp.arange(half_dim, dtype=wide) / half_dim)
        angles = positions.astype(wide)[:, None] * frequency[None, :]
        cosine, sine_table = jnp.cos(angles)[:, None, :], jnp.sin(angles)[:, None, :]
        causal = (positions[None, :] <= positions[:, None])[None]

        normed_in, unit_in, inv_in = rms_norm(layer_input, scales[0])
        attn_near, attn_far = wires.rows_all(normed_in.astype(low))
        attn_in = jnp.concatenate([attn_near, attn_far], axis=0)
        heads_q = q_width // HD
        heads_k = kv_width // HD
        qkv = dot(attn_in, full_qkv)
        query_heads = (
            rotate(qkv[:, :q_width].reshape(seq_len, heads_q, HD), cosine, sine_table) * query_mult
        ).astype(low)
        key_heads = rotate(
            qkv[:, q_width : q_width + kv_width].reshape(seq_len, heads_k, HD), cosine, sine_table
        ).astype(low)
        value_heads = qkv[:, q_width + kv_width :].reshape(seq_len, heads_k, HD).astype(low)
        attn_out, log_total = attend(query_heads, key_heads, value_heads, causal)
        attn_flat = attn_out.reshape(seq_len, q_width)
        half_rows = seq_len // 2
        mixed = wires.rows_sum(
            dot_bt(attn_flat[:half_rows], full_out), dot_bt(attn_flat[half_rows:], full_out)
        )
        post_attn, unit_mix, inv_mix = rms_norm(mixed, scales[1])
        residual = layer_input + post_attn
        normed_ff, unit_ff, inv_ff = rms_norm(residual, scales[2])
        ffn_parts = wires.rows_all(normed_ff.astype(low))
        ffn_in = jnp.concatenate(ffn_parts, axis=0)
        gates = [dot(part, full_gate) for part in ffn_parts]
        ups = [dot(part, full_up) for part in ffn_parts]
        acts = [gelu_parts(gate) for gate in gates]
        hiddens = [(act[0] * up).astype(low) for act, up in zip(acts, ups)]
        ffn_out = wires.rows_sum(*[dot_bt(hidden, full_down) for hidden in hiddens])
        post_ffn, unit_ffn, inv_ffn = rms_norm(ffn_out, scales[3])
        layer_output = residual + post_ffn

        grad_ffn, scale_three = norm_back(unit_ffn, inv_ffn, scales[3], out_grad)
        grad_ffn_parts = wires.rows_all(grad_ffn.astype(low))
        grad_ffn_all = jnp.concatenate(grad_ffn_parts, axis=0)
        hidden_all = jnp.concatenate(hiddens, axis=0)
        down_part = dot_at(grad_ffn_all, hidden_all).astype(low)
        summed_down_t = wires.scatter(down_part, True)
        grad_hiddens = [dot(part, full_down) for part in grad_ffn_parts]
        grad_gates = [
            (gh * up * act[1]).astype(low) for gh, up, act in zip(grad_hiddens, ups, acts)
        ]
        grad_ups = [(gh * act[0]).astype(low) for gh, act in zip(grad_hiddens, acts)]
        gate_part = dot_at(ffn_in, jnp.concatenate(grad_gates, axis=0)).astype(low)
        up_part = dot_at(ffn_in, jnp.concatenate(grad_ups, axis=0)).astype(low)
        summed_gate = wires.scatter(gate_part, False)
        summed_up = wires.scatter(up_part, True)
        grad_normed_ff = wires.rows_sum(
            *[
                dot_bt(gg, full_gate) + dot_bt(gu, full_up)
                for gg, gu in zip(grad_gates, grad_ups)
            ]
        )
        grad_res_ff, scale_two = norm_back(unit_ff, inv_ff, scales[2], grad_normed_ff)
        grad_residual = out_grad + grad_res_ff
        grad_mixed, scale_one = norm_back(unit_mix, inv_mix, scales[1], grad_residual)
        grad_mixed_all = jnp.concatenate(wires.rows_all(grad_mixed.astype(low)), axis=0)
        grad_attn = dot(grad_mixed_all, full_out).astype(low).reshape(seq_len, heads_q, HD)
        out_part = dot_at(grad_mixed_all, attn_flat).astype(low)
        summed_out_t = wires.scatter(out_part, False)
        grad_q, grad_k, grad_v = attend_back(
            query_heads, key_heads, value_heads, attn_out, log_total, grad_attn, causal
        )
        grad_qkv = jnp.concatenate(
            [
                rotate_back(grad_q * query_mult, cosine, sine_table)
                .astype(low)
                .reshape(seq_len, q_width),
                rotate_back(grad_k, cosine, sine_table).astype(low).reshape(seq_len, kv_width),
                grad_v.astype(low).reshape(seq_len, kv_width),
            ],
            axis=1,
        )
        qkv_part = dot_at(attn_in, grad_qkv).astype(low)
        summed_qkv = wires.scatter(qkv_part, True)
        grad_normed_in = wires.rows_sum(
            dot_bt(grad_qkv[:half_rows], full_qkv), dot_bt(grad_qkv[half_rows:], full_qkv)
        )
        grad_in_norm, scale_zero = norm_back(unit_in, inv_in, scales[0], grad_normed_in)
        input_grad = grad_residual + grad_in_norm
        scale_part = jnp.stack([scale_zero, scale_one, scale_two, scale_three])
        grad_scales = lax.dynamic_slice(
            wires.sum_all(scale_part),
            (0, my_index * scale_width),
            (norm_scales.shape[0], scale_width),
        )

        summed_query = summed_qkv[:, :q_width]
        summed_keyval = summed_qkv[:, q_width:].reshape(w_keyval.shape)
        summed_output = jnp.transpose(summed_out_t)
        summed_down = jnp.transpose(summed_down_t)
        summed_gateup = jnp.stack([summed_gate, summed_up], axis=1)
        early = wires.sum_all(
            jnp.stack([square_sum(summed_gate) + square_sum(summed_up), square_sum(summed_down_t)])
        )
        late = wires.sum_all(
            jnp.stack(
                [
                    square_sum(summed_qkv[:, :q_width]),
                    square_sum(summed_qkv[:, q_width:]),
                    square_sum(summed_out_t),
                    square_sum(grad_scales),
                ]
            )
        )
        new_q = adam_step(
            w_query, momentum_query, variance_query, clip_with(summed_query, late[0], D * HQ * HD)
        )
        new_kv = adam_step(
            w_keyval,
            momentum_keyval,
            variance_keyval,
            clip_with(summed_keyval, late[1], D * 2 * HK * HD),
        )
        new_o = adam_step(
            w_output,
            momentum_output,
            variance_output,
            clip_with(summed_output, late[2], HQ * HD * D),
        )
        new_gu = adam_step(
            w_gateup,
            momentum_gateup,
            variance_gateup,
            clip_with(summed_gateup, early[0], D * 2 * FF),
        )
        new_d = adam_step(
            w_down, momentum_down, variance_down, clip_with(summed_down, early[1], FF * D)
        )
        new_s = adam_step(
            norm_scales, momentum_scales, variance_scales, clip_with(grad_scales, late[3], 4 * D)
        )
        return (
            layer_output,
            input_grad,
            summed_query,
            summed_keyval,
            summed_output,
            summed_gateup,
            summed_down,
            grad_scales,
            new_q[0],
            new_kv[0],
            new_o[0],
            new_gu[0],
            new_d[0],
            new_s[0],
            new_q[1],
            new_kv[1],
            new_o[1],
            new_gu[1],
            new_d[1],
            new_s[1],
            new_q[2],
            new_kv[2],
            new_o[2],
            new_gu[2],
            new_d[2],
            new_s[2],
        )

    return body


def solution(mesh):
    rows = P(("dp", "tensor"), None)
    weights = (
        P("dp", "tensor"),
        P("dp", None, "tensor"),
        P("tensor", "dp"),
        P("dp", None, "tensor"),
        P("tensor", "dp"),
        P(None, ("dp", "tensor")),
    )
    return jax.shard_map(
        make_body(mesh),
        mesh=mesh,
        in_specs=(rows, rows) + weights * 3,
        out_specs=(rows, rows) + weights * 4,
        check_vma=False,
    )
```
